32 devices in a mesh: shard: 4 (over y, x), ctx: 8 (over z, core).
Axes of the slice: x: 2, y: 2, z: 4, core: 2. Of those that a mesh axis runs over, the one named last changes fastest.
Arguments:
- tokens: bfloat16 [4, 1024, 768], P('shard', 'ctx'), may hold values from -60 to 60
- lengths: int32 [4], P('shard'), may hold values from 128 to 1024, as said below
- cotangent: bfloat16 [4, 1024, 768], P('shard', 'ctx'), may hold values from -6 to 6
- w_qkv: bfloat16 [768, 2304], P('shard'), may hold values from -0.21875 to 0.21875
- b_query: bfloat16 [768], P('shard'), may hold values from -3 to 3
- b_value: bfloat16 [768], P('shard'), may hold values from -3 to 3
- w_out: bfloat16 [768, 768], P('shard'), may hold values from -3.5 to 3.5
- b_out: bfloat16 [768], P('shard'), may hold values from -3 to 3
- ln1_gain: bfloat16 [768], P('shard'), may hold values from 0.25 to 1.75
- ln1_bias: bfloat16 [768], P('shard'), may hold values from -3 to 3
- w_up: bfloat16 [768, 3072], P('shard'), may hold values from -0.21875 to 0.21875
- b_up: bfloat16 [3072], P('shard'), may hold values from -3 to 3
- w_down: bfloat16 [3072, 768], P('shard'), may hold values from -0.109375 to 0.109375
- b_down: bfloat16 [768], P('shard'), may hold values from -3 to 3
- ln2_gain: bfloat16 [768], P('shard'), may hold values from 0.25 to 1.75
- ln2_bias: bfloat16 [768], P('shard'), may hold values from -3 to 3
Outputs:
- output: bfloat16 [4, 1024, 768], P('shard', 'ctx')
- tokens_grad: float32 [4, 1024, 768], P('shard', 'ctx')
- w_qkv_grad: float32 [768, 2304], P('shard')
- b_query_grad: float32 [768], P('shard')
- b_value_grad: float32 [768], P('shard')
- w_out_grad: float32 [768, 768], P('shard')
- b_out_grad: float32 [768], P('shard')
- ln1_gain_grad: float32 [768], P('shard')
- ln1_bias_grad: float32 [768], P('shard')
- w_up_grad: float32 [768, 3072], P('shard')
- b_up_grad: float32 [3072], P('shard')
- w_down_grad: float32 [3072, 768], P('shard')
- b_down_grad: float32 [768], P('shard')
- ln2_gain_grad: float32 [768], P('shard')
- ln2_bias_grad: float32 [768], P('shard')
The draws below stay inside these ranges and needn't reach their ends.
Inputs may be any that keep to these rules, and one draw needn't show every extreme that they name: `lengths`: each sequence has at least one valid token; some sequence is entirely valid.
All inputs are finite; a program needn't handle non-finite values.
Results may differ from the reference program's by a relative error of at most 0.035.
The reference program's roundings to bfloat16 on the way count: a program that leaves them out, or rounds other values in their place, can miss the bound.
Values may be sent and summed in bfloat16 or wider, within the bound.
A program may use at most 128 MiB of HBM per device.

```python
import math
import jax
import jax.numpy as jnp
from jax import lax

D = 768
HEADS = 12
FF = 3072
HEAD_WIDTH = 64
TOK_DEV = 128
LENGTH = 1024
SEQS = 4
N_CTX = 8


def draw_tokens(key, part):
    base = jax.random.truncated_normal(key, -6.0, 6.0, (SEQS, LENGTH, D), jnp.float32)
    return base.astype(jnp.bfloat16)


def draw_lengths(key, part):
    lowest = max(1, LENGTH // 8)
    drawn = jax.random.randint(key, (SEQS,), lowest, LENGTH + 1, jnp.int32)
    where_full = jax.random.randint(jax.random.fold_in(key, 3), (), 0, SEQS, jnp.int32)
    return drawn.at[where_full].set(LENGTH)


def shard_levels(stream_key, extent, split, least, largest):
    def one(axis_at, blocks):
        heights = jax.random.uniform(jax.random.fold_in(jax.random.fold_in(stream_key, 6), axis_at), (blocks,), jnp.float32, least / len(split), largest / len(split))
        return jnp.repeat(jnp.exp(heights), extent[axis_at] // blocks).reshape((-1,) + (1,) * (len(extent) - axis_at - 1))

    level = one(*split[0])
    for cut in split[1:]:
        level = level * one(*cut)
    return level


def normal_values(own_key, shape, deviation, bound, split=(), held_as=jnp.bfloat16):
    result = deviation * jax.random.normal(own_key, shape, jnp.float32)
    if split:
        result = result * shard_levels(own_key, shape, split, -0.22, 0.18)
    return jnp.clip(result, -bound, bound).astype(held_as)


def setup_inputs(seed: int = 0) -> dict:
    arg_keys = jax.random.split(jax.random.key(seed), 17)
    tokens = draw_tokens(jax.random.fold_in(arg_keys[16], 71), 0)
    lengths = draw_lengths(jax.random.fold_in(arg_keys[16], 71), 0)
    cotangent = normal_values(arg_keys[2], (SEQS, LENGTH, D), 1.0, 6.0, ((0, 4), (1, 8)))
    w_qkv = normal_values(arg_keys[3], (D, 3 * D), D ** -0.5, 0.21875, ((0, 4),))
    b_query = normal_values(arg_keys[4], (D,), 0.5, 3.0, ((0, 4),))
    b_value = normal_values(arg_keys[5], (D,), 0.5, 3.0, ((0, 4),))
    w_out = normal_values(arg_keys[6], (D, D), (max(1, D * 4 // (TOK_DEV * N_CTX))) ** -0.5, 3.5, ((0, 4),))
    b_out = normal_values(arg_keys[7], (D,), 0.5, 3.0, ((0, 4),))
    ln1_gain = jnp.clip(1.0 + 0.15 * jax.random.normal(arg_keys[8], (D,), jnp.float32), 0.25, 1.75).astype(jnp.bfloat16)
    ln1_bias = normal_values(arg_keys[9], (D,), 0.5, 3.0, ((0, 4),))
    w_up = normal_values(arg_keys[10], (D, FF), D ** -0.5, 0.21875, ((0, 4),))
    b_up = normal_values(arg_keys[11], (FF,), 0.5, 3.0, ((0, 4),))
    w_down = normal_values(arg_keys[12], (FF, D), FF ** -0.5, 0.109375, ((0, 4),))
    b_down = normal_values(arg_keys[13], (D,), 0.5, 3.0, ((0, 4),))
    ln2_gain = jnp.clip(1.0 + 0.15 * jax.random.normal(arg_keys[14], (D,), jnp.float32), 0.25, 1.75).astype(jnp.bfloat16)
    ln2_bias = normal_values(arg_keys[15], (D,), 0.5, 3.0, ((0, 4),))
    return {"tokens": tokens, "lengths": lengths, "cotangent": cotangent, "w_qkv": w_qkv, "b_query": b_query, "b_value": b_value, "w_out": w_out, "b_out": b_out, "ln1_gain": ln1_gain, "ln1_bias": ln1_bias, "w_up": w_up, "b_up": b_up, "w_down": w_down, "b_down": b_down, "ln2_gain": ln2_gain, "ln2_bias": ln2_bias}


EPS = 1e-06

def normalize(z):
    centre = z - lax.optimization_barrier(jnp.mean(z, axis=-1, keepdims=True))
    rstd = lax.rsqrt(lax.optimization_barrier(jnp.mean(centre * centre, axis=-1, keepdims=True)) + EPS)
    return (centre * rstd, rstd)

def norm_back(dnorm, normed, rstd):
    return rstd * (dnorm - lax.optimization_barrier(jnp.mean(dnorm, axis=-1, keepdims=True)) - normed * lax.optimization_barrier(jnp.mean(dnorm * normed, axis=-1, keepdims=True)))

def gelu_exact(t):
    return jax.nn.gelu(t, approximate=False)

def leading_product(left, right):
    return lax.dot_general(left, right, (((0,), (0,)), ((), ())), preferred_element_type=jnp.float32)

def dot_last(left, right):
    return lax.dot_general(left, right, (((1,), (1,)), ((), ())), preferred_element_type=jnp.float32)

def reference(tokens, lengths, cotangent, w_qkv, b_query, b_value, w_out, b_out, ln1_gain, ln1_bias, w_up, b_up, w_down, b_down, ln2_gain, ln2_bias):
    single_float = jnp.float32
    bf16 = jnp.bfloat16
    scale = 1.0 / math.sqrt(HEAD_WIDTH)
    block_rows = math.gcd(LENGTH, 512)
    token_count = LENGTH // block_rows
    positions = jnp.arange(LENGTH, dtype=jnp.int32)
    bq, bv, bo = (b_query.astype(single_float), b_value.astype(single_float), b_out.astype(single_float))
    g1, c1, bu = (ln1_gain.astype(single_float), ln1_bias.astype(single_float), b_up.astype(single_float))
    bd, g2, c2 = (b_down.astype(single_float), ln2_gain.astype(single_float), ln2_bias.astype(single_float))

    def split_heads(a):
        return a.reshape(a.shape[0], HEADS, HEAD_WIDTH).transpose(1, 0, 2)

    def merge_heads(a):
        return a.transpose(1, 0, 2).reshape(a.shape[1], HEADS * HEAD_WIDTH)

    def one_sequence(carry, item):
        x, limit, dy = item
        valid = positions < limit
        qkv = jnp.dot(x, w_qkv, preferred_element_type=single_float)
        query = (qkv[:, :D] + bq).astype(bf16)
        keys = qkv[:, D:2 * D].astype(bf16)
        values = (qkv[:, 2 * D:] + bv).astype(bf16)
        qh, kh, vh = (split_heads(query), split_heads(keys), split_heads(values))

        def head_fwd(operations):
            query_index, key_index, value_index = operations

            def token_block(qpart):
                scores = jnp.dot(qpart, key_index.T, preferred_element_type=single_float) * scale
                scores = jnp.where(valid[None, :], scores, -1e+30)
                peak = lax.optimization_barrier(jnp.max(scores, axis=1, keepdims=True))
                lse = peak + jnp.log(lax.optimization_barrier(jnp.sum(jnp.exp(scores - peak), axis=1, keepdims=True)))
                probs = jnp.exp(scores - lse).astype(bf16)
                return (jnp.dot(probs, value_index, preferred_element_type=single_float), lse[:, 0])
            ctx_part, lse_part = lax.map(token_block, query_index.reshape(token_count, block_rows, HEAD_WIDTH))
            return (ctx_part.reshape(LENGTH, HEAD_WIDTH), lse_part.reshape(LENGTH))
        ctx_heads, lse_all = lax.map(head_fwd, (qh, kh, vh))
        context = merge_heads(ctx_heads)
        context_b = context.astype(bf16)
        z_one = x.astype(single_float) + jnp.dot(context_b, w_out, preferred_element_type=single_float) + bo
        n_one, rstd_one = normalize(z_one)
        x_one = n_one * g1 + c1
        x_one_b = x_one.astype(bf16)
        upper = jnp.dot(x_one_b, w_up, preferred_element_type=single_float) + bu
        hidden_f, gelu_back = jax.vjp(gelu_exact, upper)
        hidden = hidden_f.astype(bf16)
        z_two = x_one + jnp.dot(hidden, w_down, preferred_element_type=single_float) + bd
        n_two, rstd_two = normalize(z_two)
        out = (n_two * g2 + c2).astype(bf16)
        grad = dy.astype(single_float)
        dg_two = lax.optimization_barrier(jnp.sum(grad * n_two, axis=0))
        db_two = lax.optimization_barrier(jnp.sum(grad, axis=0))
        dz_two = norm_back(grad * g2, n_two, rstd_two)
        dz_two_b = dz_two.astype(bf16)
        dw_down = leading_product(hidden, dz_two_b)
        db_down = lax.optimization_barrier(jnp.sum(dz_two, axis=0))
        dhid = dot_last(dz_two_b, w_down)
        dupper = gelu_back(dhid)[0]
        dupper_b = dupper.astype(bf16)
        dw_up = leading_product(x_one_b, dupper_b)
        db_up = lax.optimization_barrier(jnp.sum(dupper, axis=0))
        dx_one = dz_two + dot_last(dupper_b, w_up)
        dg_one = lax.optimization_barrier(jnp.sum(dx_one * n_one, axis=0))
        db_one = lax.optimization_barrier(jnp.sum(dx_one, axis=0))
        dz_one = norm_back(dx_one * g1, n_one, rstd_one)
        dz_one_b = dz_one.astype(bf16)
        dw_out = leading_product(context_b, dz_one_b)
        db_out = lax.optimization_barrier(jnp.sum(dz_one, axis=0))
        dctx = dot_last(dz_one_b, w_out)
        dctx_b = dctx.astype(bf16)
        delta = lax.optimization_barrier(jnp.sum(split_heads(dctx) * ctx_heads, axis=2))
        dch = split_heads(dctx_b)

        def head_bwd(operations):
            query_index, key_index, value_index, lse_index, context_grad_index, delta_index = operations

            def token_block(acc, pieces):
                qpart, lpart, dpart, epart = pieces
                scores = jnp.dot(qpart, key_index.T, preferred_element_type=single_float) * scale
                scores = jnp.where(valid[None, :], scores, -1e+30)
                prob = jnp.exp(scores - lpart[:, None])
                block_probs = prob.astype(bf16)
                value_gradient = acc[1] + leading_product(block_probs, dpart)
                prob_gradient = jnp.dot(dpart, value_index.T, preferred_element_type=single_float)
                dscore = (prob * (prob_gradient - epart[:, None])).astype(bf16)
                query_gradient = jnp.dot(dscore, key_index, preferred_element_type=single_float) * scale
                key_gradient = acc[0] + leading_product(dscore, qpart) * scale
                return ((key_gradient, value_gradient), query_gradient)
            zero_filled = jnp.zeros((LENGTH, HEAD_WIDTH), single_float)
            (key_gradient, value_gradient), query_gradient = lax.scan(token_block, (zero_filled, zero_filled), (query_index.reshape(token_count, block_rows, HEAD_WIDTH), lse_index.reshape(token_count, block_rows), context_grad_index.reshape(token_count, block_rows, HEAD_WIDTH), delta_index.reshape(token_count, block_rows)))
            return (query_gradient.reshape(LENGTH, HEAD_WIDTH), key_gradient, value_gradient)
        dqh, dkh, dvh = lax.map(head_bwd, (qh, kh, vh, lse_all, dch, delta))
        query_gradient, key_gradient, value_gradient = (merge_heads(dqh), merge_heads(dkh), merge_heads(dvh))
        dqkv_b = jnp.concatenate([query_gradient, key_gradient, value_gradient], axis=1).astype(bf16)
        dw_qkv = leading_product(x, dqkv_b)
        dx = dz_one + dot_last(dqkv_b, w_qkv)
        terms = (dw_qkv, lax.optimization_barrier(jnp.sum(query_gradient, axis=0)), lax.optimization_barrier(jnp.sum(value_gradient, axis=0)), dw_out, db_out, dg_one, db_one, dw_up, db_up, dw_down, db_down, dg_two, db_two)
        carry = tuple((a + b for a, b in zip(carry, terms)))
        return (carry, (out, dx))
    start = (jnp.zeros((D, 3 * D), single_float), jnp.zeros((D,), single_float), jnp.zeros((D,), single_float), jnp.zeros((D, D), single_float), jnp.zeros((D,), single_float), jnp.zeros((D,), single_float), jnp.zeros((D,), single_float), jnp.zeros((D, FF), single_float), jnp.zeros((FF,), single_float), jnp.zeros((FF, D), single_float), jnp.zeros((D,), single_float), jnp.zeros((D,), single_float), jnp.zeros((D,), single_float))
    grads, (outs, dxs) = lax.scan(one_sequence, start, (tokens, lengths, cotangent))
    return (outs, dxs, grads[0], grads[1], grads[2], grads[3], grads[4], grads[5], grads[6], grads[7], grads[8], grads[9], grads[10], grads[11], grads[12])
```

```python
import functools
import math

import jax
import jax.numpy as jnp
from jax import lax
from jax.experimental import pallas as pl
from jax.experimental.pallas import tpu as pltpu
from jax.sharding import PartitionSpec as P

HEADS = 12
EPS = 1e-06
MESH = pl.DeviceIdType.MESH
F32 = jnp.float32
BF16 = jnp.bfloat16
VMEM_LIMIT = 60 * 1024 * 1024


def normalize(z):
    centre = z - jnp.mean(z, axis=-1, keepdims=True)
    rstd = lax.rsqrt(jnp.mean(centre * centre, axis=-1, keepdims=True) + EPS)
    return (centre * rstd, rstd)


def norm_back(dnorm, normed, rstd):
    return rstd * (
        dnorm
        - jnp.mean(dnorm, axis=-1, keepdims=True)
        - normed * jnp.mean(dnorm * normed, axis=-1, keepdims=True)
    )


def gelu_exact(t):
    return jax.nn.gelu(t, approximate=False)


def contract_dims(left, right, left_dim, right_dim):
    return lax.dot_general(
        left, right, (((left_dim,), (right_dim,)), ((), ())), preferred_element_type=F32
    )


class Place:
    def __init__(self, n):
        self.n = n
        self.s = lax.axis_index("shard")
        self.c = lax.axis_index("ctx")
        self.core = lax.rem(self.c, 2)
        self.m = lax.div(self.c, 2)
        self.sib = self.m * 2 + (1 - self.core)
        self.p = self.flip(self.s)
        self.right = self.at(1)
        self.left = self.at(-1)

    def flip(self, q):
        half = self.n // 2
        return jnp.where(q < half, q, 3 * half - 1 - q)

    def at(self, offset):
        return self.flip(lax.rem(self.p + (offset % self.n), self.n))


def greet(peers):
    barrier = pltpu.get_barrier_semaphore()
    for peer in peers:
        pl.semaphore_signal(barrier, inc=1, device_id=peer, device_id_type=MESH)
    pl.semaphore_wait(barrier, len(peers))


def remote(src, dst, send, recv, peer):
    return pltpu.make_async_remote_copy(
        src_ref=src, dst_ref=dst, send_sem=send, recv_sem=recv, device_id=peer, device_id_type=MESH
    )


def gather_kernel(n, pairs, nw, small, kv, *refs):
    total = nw + int(small) + int(kv)
    ins, outs, sems = refs[:total], refs[total : 2 * total], refs[2 * total :]
    send, recv, dsend, drecv, lsem, ssend, srecv, ksend, krecv, esend, erecv = sems
    here = Place(n)
    s, c, m, core = here.s, here.c, here.m, here.core
    across = [(s, lax.rem(m + k, pairs) * 2 + core) for k in range(1, pairs)] if kv else []
    greet([(here.right, c), (here.left, c), (s, here.sib)] + across)

    def key(i, d, t):
        return (i * 2 + d) * (n - 1) + t

    def part(i, d, block=None):
        rows, cols = ins[i].shape
        where = (pl.ds(pl.multiple_of(core * (rows // 2), rows // 2), rows // 2),
                 pl.ds(d * (cols // 2), cols // 2))
        return ins[i].at[where] if block is None else outs[i].at[(block,) + where]

    def ring(i, d, t):
        owner = here.at(-t if d == 0 else t)
        k = key(i, d, t)
        return remote(
            part(i, d) if t == 0 else part(i, d, owner),
            part(i, d, owner),
            send.at[k], recv.at[k],
            (here.right if d == 0 else here.left, c),
        )

    def pair(i, d, t):
        owner = here.at(-1 - t if d == 0 else 1 + t)
        k = key(i, d, t)
        return remote(part(i, d, owner), part(i, d, owner), dsend.at[k], drecv.at[k], (s, here.sib))

    def small_ring(t):
        owner = here.at(-t)
        return remote(
            ins[nw] if t == 0 else outs[nw].at[owner],
            outs[nw].at[owner],
            ssend.at[t], srecv.at[t],
            (here.right, c),
        )

    kin, kout = ins[-1], outs[-1]

    def kv_send(k):
        return remote(kin, kout.at[c], ksend.at[k - 1], krecv.at[k - 1], across[k - 1])

    def kv_pair(k):
        block = lax.rem(m + pairs - k, pairs) * 2 + core
        return remote(
            kin if k == 0 else kout.at[block], kout.at[block], esend.at[k], erecv.at[k], (s, here.sib)
        )

    local = [
        pltpu.make_async_copy(ins[i], outs[i].at[c if kv and i == total - 1 else s], lsem.at[i])
        for i in range(total)
    ]
    if kv:
        for k in range(1, pairs):
            kv_send(k).start()
        kv_pair(0).start()
    if small:
        small_ring(0).start()
    for i in range(nw):
        for d in range(2):
            ring(i, d, 0).start()
    for copy in local:
        copy.start()
    for t in range(n - 1):
        if small:
            small_ring(t).wait_recv()
            if t + 1 < n - 1:
                small_ring(t + 1).start()
        for i in range(nw):
            for d in range(2):
                ring(i, d, t).wait_recv()
                if t + 1 < n - 1:
                    ring(i, d, t + 1).start()
                pair(i, d, t).start()
    if kv:
        for k in range(1, pairs):
            kv_send(k).wait_recv()
            kv_pair(k).start()
    for copy in local:
        copy.wait()
    for t in range(n - 1):
        if small:
            small_ring(t).wait_send()
        for i in range(nw):
            for d in range(2):
                ring(i, d, t).wait_send()
                pair(i, d, t).wait()
    if kv:
        for k in range(1, pairs):
            kv_send(k).wait_send()
        for k in range(pairs):
            kv_pair(k).wait()


def gather(n, pairs, cid, weights, small=None, kv=None):
    nw = len(weights)
    args = list(weights)
    shapes = [jax.ShapeDtypeStruct((n,) + w.shape, w.dtype) for w in weights]
    if small is not None:
        args.append(small)
        shapes.append(jax.ShapeDtypeStruct((n,) + small.shape, small.dtype))
    if kv is not None:
        args.append(kv)
        shapes.append(jax.ShapeDtypeStruct((2 * pairs,) + kv.shape, kv.dtype))
    dma = pltpu.SemaphoreType.DMA
    count = nw * 2 * (n - 1)
    outs = pl.pallas_call(
        functools.partial(gather_kernel, n, pairs, nw, small is not None, kv is not None),
        out_shape=shapes,
        in_specs=[pl.BlockSpec(memory_space=pltpu.VMEM)] * len(args),
        out_specs=[pl.BlockSpec(memory_space=pl.ANY)] * len(args),
        scratch_shapes=[dma((count,))] * 4
        + [dma((len(args),))]
        + [dma((n - 1,))] * 2
        + [dma((pairs,))] * 4,
        compiler_params=pltpu.CompilerParams(
            collective_id=cid, has_side_effects=True, vmem_limit_bytes=VMEM_LIMIT
        ),
        name=f"gather{cid}",
    )(*args)
    return list(outs)


def add_into(dst, sources, rows, cols, chunk=16):
    def view(item, r):
        ref, lead, row0, col0 = item
        start = pl.multiple_of(row0 + r * chunk, chunk)
        return ref.at[lead + (pl.ds(start, chunk), pl.ds(col0, cols))]

    def step(r, carry):
        value = view(sources[0], r)[...].astype(F32)
        for item in sources[1:]:
            value = value + view(item, r)[...].astype(F32)
        out = view(dst, r)
        out[...] = value.astype(out.dtype)
        return carry

    lax.fori_loop(0, rows // chunk, step, 0)


def scatter_kernel(n, pairs, nw, units, kv, *refs):
    nin = nw + int(kv)
    ins, outs = refs[:nin], refs[nin : 2 * nin]
    rest = refs[2 * nin :]
    got, acc, hop, up, down = (rest[j * nw : (j + 1) * nw] for j in range(5))
    rest = rest[5 * nw :]
    if kv:
        mate, far = rest[:2]
        rest = rest[2:]
    gsend, grecv, rsend, rrecv, usend, urecv, vrecv, bsend, brecv, osend, orecv = rest[:11]
    here = Place(n)
    s, c, m, core = here.s, here.c, here.m, here.core
    sib = (s, here.sib)
    above = lax.rem(m + 1, pairs) * 2 + core
    below = lax.rem(m + pairs - 1, pairs) * 2 + core
    root = pairs // 2
    if kv:
        across = [(s, lax.rem(m + k, pairs) * 2 + core) for k in range(1, pairs)]
    else:
        across = [(s, above), (s, below)]
    greet([(here.right, c), (here.left, c), sib] + across)

    offsets = []
    for k in range(1, n // 2 + 1):
        for o in (-k, k):
            if o % n not in [q % n for q in offsets]:
                offsets.append(o)
    offsets.append(0)

    def half_rows(i):
        return ins[i].shape[1] // 2

    def mine(i):
        return pl.multiple_of(core * half_rows(i), half_rows(i))

    def theirs(i):
        return pl.multiple_of((1 - core) * half_rows(i), half_rows(i))

    def swap(i, j):
        block = here.at(offsets[j])
        k = i * n + j
        return remote(
            ins[i].at[block, pl.ds(theirs(i), half_rows(i)), :],
            got[i].at[block],
            gsend.at[k], grecv.at[k], sib,
        )

    if kv:
        din, dout = ins[-1], outs[-1]
        ksend, krecv, esend, erecv = rest[11:15]
        token_rows, token_cols = din.shape[1:]

        def kv_swap(k):
            q = lax.rem(m + k, pairs)
            return remote(din.at[q * 2 + 1 - core], mate.at[q], esend.at[k], erecv.at[k], sib)

        def kv_send(k):
            q = lax.rem(m + k, pairs)
            return remote(
                mate.at[q], far.at[k - 1], ksend.at[k - 1], krecv.at[k - 1], across[k - 1]
            )

        for k in list(range(1, pairs)) + [0]:
            kv_swap(k).start()
    for j in range(n):
        for i in range(nw):
            swap(i, j).start()
    if kv:
        for k in list(range(1, pairs)) + [0]:
            q = lax.rem(m + k, pairs)
            kv_swap(k).wait_recv()
            add_into((mate, (q,), 0, 0), [(mate, (q,), 0, 0), (din, (q * 2 + core,), 0, 0)],
                     token_rows, token_cols)
            if k:
                kv_send(k).start()
    for j in range(n):
        block = here.at(offsets[j])
        for i in range(nw):
            swap(i, j).wait_recv()
            add_into((acc[i], (block,), 0, 0),
                     [(got[i], (block,), 0, 0), (ins[i], (block,), mine(i), 0)],
                     half_rows(i), ins[i].shape[2])

    def region(k, d):
        i, piece, width = units[k]
        return i, half_rows(i), d * (ins[i].shape[2] // 2) + piece * width, width

    def ring(k, d, t):
        i, rows, col, width = region(k, d)
        block = here.at(-1 - t if d == 0 else 1 + t)
        q = (k * 2 + d) * (n - 1) + t
        return remote(
            acc[i].at[block, :, pl.ds(col, width)],
            hop[i].at[t, :, pl.ds(col, width)],
            rsend.at[q], rrecv.at[q],
            (here.right if d == 0 else here.left, c),
        )

    def own(k, d):
        i, rows, col, width = region(k, d)
        return acc[i].at[s, :, pl.ds(col, width)]

    def climb(k, d):
        i, rows, col, width = region(k, d)
        q = k * 2 + d
        return remote(own(k, d), up[i].at[:, pl.ds(col, width)], usend.at[q], urecv.at[q], (s, above))

    def descend(k, d):
        i, rows, col, width = region(k, d)
        q = k * 2 + d
        return remote(own(k, d), down[i].at[:, pl.ds(col, width)], usend.at[q], vrecv.at[q], (s, below))

    def final(k, d):
        i, rows, col, width = region(k, d)
        return outs[i].at[pl.ds(mine(i), rows), pl.ds(col, width)]

    def share(k, d, side):
        q = k * 2 + d
        return remote(
            final(k, d), final(k, d), bsend.at[q * 2 + side], brecv.at[q], (s, above if side else below)
        )

    def twin(k, d):
        q = k * 2 + d
        return remote(final(k, d), final(k, d), osend.at[q], orecv.at[q], sib)

    def ring_step(t, k, d):
        i, rows, col, width = region(k, d)
        if t >= 0:
            ring(k, d, t).wait_recv()
            block = here.at(-2 - t if d == 0 else 2 + t)
            add_into((acc[i], (block,), 0, col), [(acc[i], (block,), 0, col), (hop[i], (t,), 0, col)],
                     rows, width)
        if t + 1 < n - 1:
            ring(k, d, t + 1).start()

    def chain_step(h, k, d):
        i, rows, col, width = region(k, d)

        @pl.when((m == h) & (m < root))
        def _():
            if h > 0:
                climb(k, d).wait_recv()
                add_into((acc[i], (s,), 0, col), [(acc[i], (s,), 0, col), (up[i], (), 0, col)],
                         rows, width)
            climb(k, d).start()

        @pl.when((m == pairs - 1 - h) & (m > root))
        def _():
            if h > 0:
                descend(k, d).wait_recv()
                add_into((acc[i], (s,), 0, col), [(acc[i], (s,), 0, col), (down[i], (), 0, col)],
                         rows, width)
            descend(k, d).start()

    def root_step(k, d):
        i, rows, col, width = region(k, d)

        @pl.when(m == root)
        def _():
            items = [(acc[i], (s,), 0, col)]
            if root > 0:
                climb(k, d).wait_recv()
                items.append((up[i], (), 0, col))
            if root < pairs - 1:
                descend(k, d).wait_recv()
                items.append((down[i], (), 0, col))
            add_into((outs[i], (), mine(i), col), items, rows, width)
            if root > 0:
                share(k, d, 0).start()
            if root < pairs - 1:
                share(k, d, 1).start()
            twin(k, d).start()

    def back_step(h, k, d):
        @pl.when(m == root - h)
        def _():
            share(k, d, 0).wait_recv()
            if root - h > 0:
                share(k, d, 0).start()
            twin(k, d).start()

        @pl.when(m == root + h)
        def _():
            share(k, d, 1).wait_recv()
            if root + h < pairs - 1:
                share(k, d, 1).start()
            twin(k, d).start()

    stages = [functools.partial(ring_step, t) for t in range(-1, n - 1)]
    stages += [functools.partial(chain_step, h) for h in range(max(root, pairs - 1 - root))]
    stages += [root_step]
    stages += [functools.partial(back_step, h) for h in range(1, max(root, pairs - 1 - root) + 1)]
    for tick in range(len(units) + len(stages) - 1):
        for stage in reversed(range(len(stages))):
            k = tick - stage
            if 0 <= k < len(units):
                for d in range(2):
                    stages[stage](k, d)

    if kv:
        items = [(mate, (m,), 0, 0)]
        for k in range(1, pairs):
            kv_send(k).wait_recv()
            items.append((far, (k - 1,), 0, 0))
        add_into((dout, (), 0, 0), items, token_rows, token_cols)
        for k in range(pairs):
            kv_swap(k).wait_send()
            if k:
                kv_send(k).wait_send()
    for i in range(nw):
        for j in range(n):
            swap(i, j).wait_send()
    for k in range(len(units)):
        for d in range(2):
            for t in range(n - 1):
                ring(k, d, t).wait_send()

            @pl.when(m != root)
            def _():
                climb(k, d).wait_send()

            @pl.when((m > 0) & (m <= root))
            def _():
                share(k, d, 0).wait_send()

            @pl.when((m >= root) & (m < pairs - 1))
            def _():
                share(k, d, 1).wait_send()

            twin(k, d).wait()


def scatter(n, pairs, cid, grads, kv=None):
    nw = len(grads)
    units = []
    for i, g in enumerate(grads):
        width = g.shape[2] // 2
        pieces = 3 if width % 384 == 0 and width * g.shape[1] >= 200000 else 1
        units += [(i, j, width // pieces) for j in range(pieces)]
    args = list(grads)
    shapes = [jax.ShapeDtypeStruct(g.shape[1:], BF16) for g in grads]
    vm = pltpu.VMEM
    halves = [(g.shape[1] // 2, g.shape[2]) for g in grads]
    scratch = [vm((n,) + h, BF16) for h in halves] * 2
    scratch += [vm((n - 1,) + h, BF16) for h in halves]
    scratch += [vm(h, BF16) for h in halves] * 2
    dma = pltpu.SemaphoreType.DMA
    both = 2 * len(units)
    sems = [dma((nw * n,))] * 2 + [dma((both * (n - 1),))] * 2 + [dma((both,))] * 3
    sems += [dma((2 * both,)), dma((both,)), dma((both,)), dma((both,))]
    if kv is not None:
        args.append(kv)
        shapes.append(jax.ShapeDtypeStruct(kv.shape[1:], F32))
        scratch += [vm((pairs,) + kv.shape[1:], BF16), vm((pairs - 1,) + kv.shape[1:], BF16)]
        sems += [dma((pairs,))] * 4
    outs = pl.pallas_call(
        functools.partial(scatter_kernel, n, pairs, nw, tuple(units), kv is not None),
        out_shape=shapes,
        in_specs=[pl.BlockSpec(memory_space=pltpu.VMEM)] * len(args),
        out_specs=[pl.BlockSpec(memory_space=pltpu.VMEM)] * len(args),
        scratch_shapes=scratch + sems,
        compiler_params=pltpu.CompilerParams(
            collective_id=cid, has_side_effects=True, vmem_limit_bytes=VMEM_LIMIT
        ),
        name=f"scatter{cid}",
    )(*args)
    return list(outs)


def lanes(ref):
    return jnp.concatenate([ref[j] for j in range(ref.shape[0])], axis=1)


def attend_kernel(scale, q_ref, k_ref, v_ref, valid_ref, ctx_ref, lse_ref):
    scores = contract_dims(q_ref[...], lanes(k_ref), 0, 0) * scale
    scores = jnp.where(valid_ref[...] > 0, scores, -1e30)
    peak = jnp.max(scores, axis=1, keepdims=True)
    weight = jnp.exp(scores - peak)
    norm = jnp.sum(weight, axis=1, keepdims=True)
    lse_ref[0] = peak + jnp.log(norm)
    probs = (weight * (1.0 / norm)).astype(BF16)
    ctx_ref[...] = contract_dims(lanes(v_ref), probs, 1, 1)


def attend(scale, query_t, kv, valid):
    width, toks = query_t.shape
    size = width // HEADS
    blocks = kv.shape[0]
    return pl.pallas_call(
        functools.partial(attend_kernel, scale),
        grid=(HEADS,),
        out_shape=(
            jax.ShapeDtypeStruct((width, toks), F32),
            jax.ShapeDtypeStruct((HEADS, toks, 1), F32),
        ),
        in_specs=[
            pl.BlockSpec((size, toks), lambda h: (h, 0)),
            pl.BlockSpec((blocks, size, toks), lambda h: (0, h, 0)),
            pl.BlockSpec((blocks, size, toks), lambda h: (0, HEADS + h, 0)),
            pl.BlockSpec(valid.shape, lambda h: (0, 0)),
        ],
        out_specs=(
            pl.BlockSpec((size, toks), lambda h: (h, 0)),
            pl.BlockSpec((1, toks, 1), lambda h: (h, 0, 0)),
        ),
        compiler_params=pltpu.CompilerParams(vmem_limit_bytes=VMEM_LIMIT // 2),
        name="attend",
    )(query_t, kv, kv, valid)


def attend_back_kernel(
    scale, q_ref, k_ref, v_ref, valid_ref, lse_ref, dctx_ref, ctx_ref, dq_ref, dk_ref, dv_ref
):
    query, keys, values = q_ref[...], lanes(k_ref), lanes(v_ref)
    dctx = dctx_ref[...]
    dctx_b = dctx.astype(BF16)
    delta_row = jnp.sum(dctx * ctx_ref[...], axis=0, keepdims=True)
    delta = jnp.transpose(jnp.broadcast_to(delta_row, (8, delta_row.shape[1])))[:, :1]
    scores = contract_dims(query, keys, 0, 0) * scale
    scores = jnp.where(valid_ref[...] > 0, scores, -1e30)
    prob = jnp.exp(scores - lse_ref[0])
    dvalue = jnp.dot(dctx_b, prob.astype(BF16), preferred_element_type=F32)
    dprob = contract_dims(dctx_b, values, 0, 0)
    dscore = (prob * (dprob - delta)).astype(BF16)
    dq_ref[...] = contract_dims(keys, dscore, 1, 1) * scale
    dkey = jnp.dot(query, dscore, preferred_element_type=F32) * scale
    toks = query.shape[1]
    for j in range(dk_ref.shape[0]):
        dk_ref[j] = dkey[:, j * toks : (j + 1) * toks].astype(BF16)
        dv_ref[j] = dvalue[:, j * toks : (j + 1) * toks].astype(BF16)


def attend_back(scale, query_t, kv, valid, lse, dctx_t, ctx_t):
    width, toks = query_t.shape
    size = width // HEADS
    blocks = kv.shape[0]
    head = pl.BlockSpec((size, toks), lambda h: (h, 0))
    keys = pl.BlockSpec((blocks, size, toks), lambda h: (0, h, 0))
    return pl.pallas_call(
        functools.partial(attend_back_kernel, scale),
        grid=(HEADS,),
        out_shape=(
            jax.ShapeDtypeStruct((width, toks), F32),
            jax.ShapeDtypeStruct((blocks, width, toks), BF16),
            jax.ShapeDtypeStruct((blocks, width, toks), BF16),
        ),
        in_specs=[
            head,
            keys,
            pl.BlockSpec((blocks, size, toks), lambda h: (0, HEADS + h, 0)),
            pl.BlockSpec(valid.shape, lambda h: (0, 0)),
            pl.BlockSpec((1, toks, 1), lambda h: (h, 0, 0)),
            head,
            head,
        ],
        out_specs=(head, keys, keys),
        compiler_params=pltpu.CompilerParams(vmem_limit_bytes=VMEM_LIMIT // 2),
        name="attend_back",
    )(query_t, kv, kv, valid, lse, dctx_t, ctx_t)


def local(
    n,
    n_ctx,
    tokens,
    lengths,
    cotangent,
    w_qkv,
    b_query,
    b_value,
    w_out,
    b_out,
    ln1_gain,
    ln1_bias,
    w_up,
    b_up,
    w_down,
    b_down,
    ln2_gain,
    ln2_bias,
):
    pairs = n_ctx // 2
    x = tokens[0]
    toks, width = x.shape
    scale = 1.0 / math.sqrt(width // HEADS)
    limit = lengths[0]
    vectors = (b_query, b_value, b_out, ln1_gain, ln1_bias, b_down, ln2_gain, ln2_bias, b_up)
    lens = [v.shape[0] for v in vectors]
    flat = jnp.concatenate(vectors)
    lane = 256
    rows = -(-sum(lens) // lane)
    rows = -(-rows // 32) * 32
    flat = jnp.pad(flat, (0, rows * lane - sum(lens))).reshape(rows, lane)
    wq_all, small_all = gather(n, pairs, 0, [w_qkv], small=flat)
    wq_full = wq_all.reshape(width, -1)
    small_all = small_all.reshape(n, rows * lane)
    parts, at = [], 0
    for size in lens:
        parts.append(small_all[:, at : at + size].reshape(-1).astype(F32))
        at += size
    bq, bv, bo, g1, c1, bd, g2, c2, bu = parts

    qkv_t = contract_dims(wq_full, x, 0, 1)
    query_t = (qkv_t[:width] + bq[:, None]).astype(BF16)
    shift = jnp.concatenate([jnp.zeros((width,), F32), bv])
    kv_t = (qkv_t[width:] + shift[:, None]).astype(BF16)
    wo_all, wu_all, wd_all, kv = gather(n, pairs, 1, [w_out, w_up, w_down], kv=kv_t)
    wo_full = wo_all.reshape(width, -1)
    wu_full = wu_all.reshape(width, -1)
    wd_full = wd_all.reshape(-1, width)
    valid = (jnp.arange(n_ctx * toks, dtype=jnp.int32) < limit).astype(F32)[None, :]

    ctx_t, lse = attend(scale, query_t, kv, valid)
    context_b_t = ctx_t.astype(BF16)
    z_one = x.astype(F32) + contract_dims(context_b_t, wo_full, 0, 0) + bo
    n_one, rstd_one = normalize(z_one)
    x_one = n_one * g1 + c1
    x_one_b = x_one.astype(BF16)
    upper = jnp.dot(x_one_b, wu_full, preferred_element_type=F32) + bu
    hidden_f, gelu_back = jax.vjp(gelu_exact, upper)
    hidden = hidden_f.astype(BF16)
    z_two = x_one + jnp.dot(hidden, wd_full, preferred_element_type=F32) + bd
    n_two, rstd_two = normalize(z_two)
    out = (n_two * g2 + c2).astype(BF16)
    grad = cotangent[0].astype(F32)
    dg_two = jnp.sum(grad * n_two, axis=0)
    db_two = jnp.sum(grad, axis=0)
    dz_two = norm_back(grad * g2, n_two, rstd_two)
    dz_two_b = dz_two.astype(BF16)
    dw_down = contract_dims(hidden, dz_two_b, 0, 0)
    db_down = jnp.sum(dz_two, axis=0)
    dhid = contract_dims(dz_two_b, wd_full, 1, 1)
    dupper = gelu_back(dhid)[0]
    dupper_b = dupper.astype(BF16)
    dw_up = contract_dims(x_one_b, dupper_b, 0, 0)
    db_up = jnp.sum(dupper, axis=0)
    dx_one = dz_two + contract_dims(dupper_b, wu_full, 1, 1)
    dg_one = jnp.sum(dx_one * n_one, axis=0)
    db_one = jnp.sum(dx_one, axis=0)
    dz_one = norm_back(dx_one * g1, n_one, rstd_one)
    dz_one_b = dz_one.astype(BF16)
    dw_out = contract_dims(context_b_t, dz_one_b, 1, 0)
    db_out = jnp.sum(dz_one, axis=0)
    dctx_t = contract_dims(wo_full, dz_one_b, 1, 1)

    query_grad_t, dkeys, dvalues = attend_back(scale, query_t, kv, valid, lse, dctx_t, ctx_t)
    dkv = jnp.concatenate([dkeys, dvalues], axis=1)

    def blocks(g):
        return g.astype(BF16).reshape(n, -1, g.shape[1])

    up_sum, down_sum, out_sum, kv_grad_t = scatter(
        n, pairs, 2, [blocks(dw_up), blocks(dw_down), blocks(dw_out)], kv=dkv
    )
    dqkv_b_t = jnp.concatenate([query_grad_t.astype(BF16), kv_grad_t.astype(BF16)], axis=0)
    dw_qkv = contract_dims(x, dqkv_b_t, 0, 1)
    dx = dz_one + contract_dims(dqkv_b_t, wq_full, 0, 1)
    db_query = jnp.sum(query_grad_t, axis=1)
    db_value = jnp.sum(kv_grad_t[width:], axis=1)
    small_grads = (db_query, db_value, db_out, dg_one, db_one, db_down, dg_two, db_two, db_up)
    packed = jnp.concatenate([g.astype(BF16).reshape(n, -1) for g in small_grads], axis=1)
    packed = jnp.pad(packed, ((0, 0), (0, rows * lane - packed.shape[1]))).reshape(n, rows, lane)
    qkv_sum, small_sum = scatter(n, pairs, 3, [blocks(dw_qkv), packed])
    small_sum = small_sum.reshape(rows * lane).astype(F32)
    pieces, at = [], 0
    for size in lens:
        pieces.append(small_sum[at : at + size])
        at += size
    gq, gv, go, gg1, gc1, gd, gg2, gc2, gu = pieces
    return (
        out[None],
        dx[None],
        qkv_sum.astype(F32),
        gq,
        gv,
        out_sum.astype(F32),
        go,
        gg1,
        gc1,
        up_sum.astype(F32),
        gu,
        down_sum.astype(F32),
        gd,
        gg2,
        gc2,
    )


def solution(mesh):
    rows, blocks, flat = P("shard", None), P("shard", "ctx", None), P("shard")
    in_specs = (
        blocks, flat, blocks, rows, flat, flat, rows, flat, flat, flat, rows, flat, rows, flat, flat, flat,
    )
    out_specs = (
        blocks, blocks, rows, flat, flat, rows, flat, flat, flat, rows, flat, rows, flat, flat, flat,
    )
    body = functools.partial(local, mesh.shape["shard"], mesh.shape["ctx"])
    return jax.shard_map(body, mesh=mesh, in_specs=in_specs, out_specs=out_specs, check_vma=False)
```

```python
import functools
import math

import jax
import jax.numpy as jnp
from jax import lax
from jax.experimental import pallas as pl
from jax.experimental.pallas import tpu as pltpu
from jax.sharding import PartitionSpec as P

HEADS = 12
EPS = 1e-06
MESH = pl.DeviceIdType.MESH
F32 = jnp.float32
BF16 = jnp.bfloat16
VMEM_LIMIT = 60 * 1024 * 1024


def normalize(z):
    centre = z - jnp.mean(z, axis=-1, keepdims=True)
    rstd = lax.rsqrt(jnp.mean(centre * centre, axis=-1, keepdims=True) + EPS)
    return (centre * rstd, rstd)


def norm_back(dnorm, normed, rstd):
    return rstd * (
        dnorm
        - jnp.mean(dnorm, axis=-1, keepdims=True)
        - normed * jnp.mean(dnorm * normed, axis=-1, keepdims=True)
    )


def gelu_exact(t):
    return jax.nn.gelu(t, approximate=False)


def contract_dims(left, right, left_dim, right_dim):
    return lax.dot_general(
        left, right, (((left_dim,), (right_dim,)), ((), ())), preferred_element_type=F32
    )


class Place:
    def __init__(self, n):
        self.n = n
        self.s = lax.axis_index("shard")
        self.c = lax.axis_index("ctx")
        self.core = lax.rem(self.c, 2)
        self.m = lax.div(self.c, 2)
        self.sib = self.m * 2 + (1 - self.core)
        self.p = self.flip(self.s)
        self.right = self.at(1)
        self.left = self.at(-1)

    def flip(self, q):
        half = self.n // 2
        return jnp.where(q < half, q, 3 * half - 1 - q)

    def at(self, offset):
        return self.flip(lax.rem(self.p + (offset % self.n), self.n))


def greet(peers):
    barrier = pltpu.get_barrier_semaphore()
    for peer in peers:
        pl.semaphore_signal(barrier, inc=1, device_id=peer, device_id_type=MESH)
    pl.semaphore_wait(barrier, len(peers))


def remote(src, dst, send, recv, peer):
    return pltpu.make_async_remote_copy(
        src_ref=src, dst_ref=dst, send_sem=send, recv_sem=recv, device_id=peer, device_id_type=MESH
    )


def gather_kernel(n, pairs, nw, small, kv, *refs):
    total = nw + int(small) + int(kv)
    ins, outs, sems = refs[:total], refs[total : 2 * total], refs[2 * total :]
    send, recv, dsend, drecv, lsem, ssend, srecv, ksend, krecv, esend, erecv = sems
    here = Place(n)
    s, c, m, core = here.s, here.c, here.m, here.core
    across = [(s, lax.rem(m + k, pairs) * 2 + core) for k in range(1, pairs)] if kv else []
    greet([(here.right, c), (here.left, c), (s, here.sib)] + across)

    def key(i, d, t):
        return (i * 2 + d) * (n - 1) + t

    def part(i, d, block=None):
        rows, cols = ins[i].shape
        where = (pl.ds(pl.multiple_of(core * (rows // 2), rows // 2), rows // 2),
                 pl.ds(d * (cols // 2), cols // 2))
        return ins[i].at[where] if block is None else outs[i].at[(block,) + where]

    def ring(i, d, t):
        owner = here.at(-t if d == 0 else t)
        k = key(i, d, t)
        return remote(
            part(i, d) if t == 0 else part(i, d, owner),
            part(i, d, owner),
            send.at[k], recv.at[k],
            (here.right if d == 0 else here.left, c),
        )

    def pair(i, d, t):
        owner = here.at(-1 - t if d == 0 else 1 + t)
        k = key(i, d, t)
        return remote(part(i, d, owner), part(i, d, owner), dsend.at[k], drecv.at[k], (s, here.sib))

    def small_ring(t):
        owner = here.at(-t)
        return remote(
            ins[nw] if t == 0 else outs[nw].at[owner],
            outs[nw].at[owner],
            ssend.at[t], srecv.at[t],
            (here.right, c),
        )

    kin, kout = ins[-1], outs[-1]

    def kv_send(k):
        return remote(kin, kout.at[c], ksend.at[k - 1], krecv.at[k - 1], across[k - 1])

    def kv_pair(k):
        block = lax.rem(m + pairs - k, pairs) * 2 + core
        return remote(
            kin if k == 0 else kout.at[block], kout.at[block], esend.at[k], erecv.at[k], (s, here.sib)
        )

    local = [
        pltpu.make_async_copy(ins[i], outs[i].at[c if kv and i == total - 1 else s], lsem.at[i])
        for i in range(total)
    ]
    if kv:
        for k in range(1, pairs):
            kv_send(k).start()
        kv_pair(0).start()
    if small:
        small_ring(0).start()
    for i in range(nw):
        for d in range(2):
            ring(i, d, 0).start()
    for copy in local:
        copy.start()
    for t in range(n - 1):
        if small:
            small_ring(t).wait_recv()
            if t + 1 < n - 1:
                small_ring(t + 1).start()
        for i in range(nw):
            for d in range(2):
                ring(i, d, t).wait_recv()
                if t + 1 < n - 1:
                    ring(i, d, t + 1).start()
                pair(i, d, t).start()
    if kv:
        for k in range(1, pairs):
            kv_send(k).wait_recv()
            kv_pair(k).start()
    for copy in local:
        copy.wait()
    for t in range(n - 1):
        if small:
            small_ring(t).wait_send()
        for i in range(nw):
            for d in range(2):
                ring(i, d, t).wait_send()
                pair(i, d, t).wait()
    if kv:
        for k in range(1, pairs):
            kv_send(k).wait_send()
        for k in range(pairs):
            kv_pair(k).wait()


def gather(n, pairs, cid, weights, small=None, kv=None):
    nw = len(weights)
    args = list(weights)
    shapes = [jax.ShapeDtypeStruct((n,) + w.shape, w.dtype) for w in weights]
    if small is not None:
        args.append(small)
        shapes.append(jax.ShapeDtypeStruct((n,) + small.shape, small.dtype))
    if kv is not None:
        args.append(kv)
        shapes.append(jax.ShapeDtypeStruct((2 * pairs,) + kv.shape, kv.dtype))
    dma = pltpu.SemaphoreType.DMA
    count = nw * 2 * (n - 1)
    outs = pl.pallas_call(
        functools.partial(gather_kernel, n, pairs, nw, small is not None, kv is not None),
        out_shape=shapes,
        in_specs=[pl.BlockSpec(memory_space=pltpu.VMEM)] * len(args),
        out_specs=[pl.BlockSpec(memory_space=pl.ANY)] * len(args),
        scratch_shapes=[dma((count,))] * 4
        + [dma((len(args),))]
        + [dma((n - 1,))] * 2
        + [dma((pairs,))] * 4,
        compiler_params=pltpu.CompilerParams(
            collective_id=cid, has_side_effects=True, vmem_limit_bytes=VMEM_LIMIT
        ),
        name=f"gather{cid}",
    )(*args)
    return list(outs)


def add_into(dst, sources, rows, cols):
    fits = [k for k in range(16, rows + 1, 16) if rows % k == 0 and k * cols <= 24576]
    chunk = max(fits) if fits else 16

    def view(item, r):
        ref, lead, row0, col0 = item
        start = pl.multiple_of(row0 + r * chunk, 16)
        return ref.at[lead + (pl.ds(start, chunk), pl.ds(col0, cols))]

    def step(r, carry):
        value = view(sources[0], r)[...].astype(F32)
        for item in sources[1:]:
            value = value + view(item, r)[...].astype(F32)
        out = view(dst, r)
        out[...] = value.astype(out.dtype)
        return carry

    lax.fori_loop(0, rows // chunk, step, 0)


def scatter_kernel(n, pairs, nw, units, kv, *refs):
    nin = nw + int(kv)
    ins, outs = refs[:nin], refs[nin : 2 * nin]
    rest = refs[2 * nin :]
    got, acc, hop, up, down = (rest[j * nw : (j + 1) * nw] for j in range(5))
    rest = rest[5 * nw :]
    if kv:
        mate, far = rest[:2]
        rest = rest[2:]
    gsend, grecv, rsend, rrecv, usend, urecv, vrecv, bsend, brecv, osend, orecv = rest[:11]
    here = Place(n)
    s, c, m, core = here.s, here.c, here.m, here.core
    sib = (s, here.sib)
    above = lax.rem(m + 1, pairs) * 2 + core
    below = lax.rem(m + pairs - 1, pairs) * 2 + core
    root = pairs // 2
    if kv:
        across = [(s, lax.rem(m + k, pairs) * 2 + core) for k in range(1, pairs)]
    else:
        across = [(s, above), (s, below)]
    greet([(here.right, c), (here.left, c), sib] + across)

    def half_rows(i):
        return ins[i].shape[1] // 2

    def mine(i):
        return pl.multiple_of(core * half_rows(i), half_rows(i))

    def theirs(i):
        return pl.multiple_of((1 - core) * half_rows(i), half_rows(i))

    def region(k, d):
        i, piece, width = units[k]
        return i, half_rows(i), d * (ins[i].shape[2] // 2) + piece * width, width

    def reach(d, j):
        return here.at(-1 - j if d == 0 else 1 + j)

    def swap(k, d, j):
        i, rows, col, width = region(k, d)
        block = reach(d, j)
        q = (k * 2 + d) * n + j
        return remote(
            ins[i].at[block, pl.ds(theirs(i), rows), pl.ds(col, width)],
            got[i].at[block, :, pl.ds(col, width)],
            gsend.at[q], grecv.at[q], sib,
        )

    if kv:
        din, dout = ins[-1], outs[-1]
        ksend, krecv, esend, erecv = rest[11:15]
        token_rows, token_cols = din.shape[1:]

        def kv_swap(k):
            q = lax.rem(m + k, pairs)
            return remote(din.at[q * 2 + 1 - core], mate.at[q], esend.at[k], erecv.at[k], sib)

        def kv_send(k):
            q = lax.rem(m + k, pairs)
            return remote(
                mate.at[q], far.at[k - 1], ksend.at[k - 1], krecv.at[k - 1], across[k - 1]
            )

        def kv_step(k):
            q = lax.rem(m + k, pairs)
            kv_swap(k).wait_recv()
            add_into((mate, (q,), 0, 0), [(mate, (q,), 0, 0), (din, (q * 2 + core,), 0, 0)],
                     token_rows, token_cols)
            if k:
                kv_send(k).start()

    kv_order = list(range(1, pairs)) + [0] if kv else []
    swaps = sorted((k + j, k, j) for k in range(len(units)) for j in range(n))
    for rank, (tick, k, j) in enumerate(swaps):
        if rank == min(3, len(swaps) - 1):
            for b in kv_order:
                kv_swap(b).start()
        for d in range(2):
            swap(k, d, j).start()

    def ring(k, d, t):
        i, rows, col, width = region(k, d)
        block = here.at(-1 - t if d == 0 else 1 + t)
        q = (k * 2 + d) * (n - 1) + t
        return remote(
            acc[i].at[block, :, pl.ds(col, width)],
            hop[i].at[t, :, pl.ds(col, width)],
            rsend.at[q], rrecv.at[q],
            (here.right if d == 0 else here.left, c),
        )

    def own(k, d):
        i, rows, col, width = region(k, d)
        return acc[i].at[s, :, pl.ds(col, width)]

    def climb(k, d):
        i, rows, col, width = region(k, d)
        q = k * 2 + d
        return remote(own(k, d), up[i].at[:, pl.ds(col, width)], usend.at[q], urecv.at[q], (s, above))

    def descend(k, d):
        i, rows, col, width = region(k, d)
        q = k * 2 + d
        return remote(own(k, d), down[i].at[:, pl.ds(col, width)], usend.at[q], vrecv.at[q], (s, below))

    def final(k, d):
        i, rows, col, width = region(k, d)
        return outs[i].at[pl.ds(mine(i), rows), pl.ds(col, width)]

    def share(k, d, side):
        q = k * 2 + d
        return remote(
            final(k, d), final(k, d), bsend.at[q * 2 + side], brecv.at[q], (s, above if side else below)
        )

    def twin(k, d):
        q = k * 2 + d
        return remote(final(k, d), final(k, d), osend.at[q], orecv.at[q], sib)

    def ring_step(t, k, d):
        i, rows, col, width = region(k, d)
        block = reach(d, t + 1)
        swap(k, d, t + 1).wait_recv()
        items = [(got[i], (block,), 0, col), (ins[i], (block,), mine(i), col)]
        if t >= 0:
            ring(k, d, t).wait_recv()
            items.append((hop[i], (t,), 0, col))
        add_into((acc[i], (block,), 0, col), items, rows, width)
        if t + 1 < n - 1:
            ring(k, d, t + 1).start()

    def chain_step(h, k, d):
        i, rows, col, width = region(k, d)

        @pl.when((m == h) & (m < root))
        def _():
            if h > 0:
                climb(k, d).wait_recv()
                add_into((acc[i], (s,), 0, col), [(acc[i], (s,), 0, col), (up[i], (), 0, col)],
                         rows, width)
            climb(k, d).start()

        @pl.when((m == pairs - 1 - h) & (m > root))
        def _():
            if h > 0:
                descend(k, d).wait_recv()
                add_into((acc[i], (s,), 0, col), [(acc[i], (s,), 0, col), (down[i], (), 0, col)],
                         rows, width)
            descend(k, d).start()

    def root_step(k, d):
        i, rows, col, width = region(k, d)

        @pl.when(m == root)
        def _():
            items = [(acc[i], (s,), 0, col)]
            if root > 0:
                climb(k, d).wait_recv()
                items.append((up[i], (), 0, col))
            if root < pairs - 1:
                descend(k, d).wait_recv()
                items.append((down[i], (), 0, col))
            add_into((outs[i], (), mine(i), col), items, rows, width)
            if root > 0:
                share(k, d, 0).start()
            if root < pairs - 1:
                share(k, d, 1).start()
            twin(k, d).start()

    def back_step(h, k, d):
        @pl.when(m == root - h)
        def _():
            share(k, d, 0).wait_recv()
            if root - h > 0:
                share(k, d, 0).start()
            twin(k, d).start()

        @pl.when(m == root + h)
        def _():
            share(k, d, 1).wait_recv()
            if root + h < pairs - 1:
                share(k, d, 1).start()
            twin(k, d).start()

    stages = [functools.partial(ring_step, t) for t in range(-1, n - 1)]
    stages += [functools.partial(chain_step, h) for h in range(max(root, pairs - 1 - root))]
    stages += [root_step]
    stages += [functools.partial(back_step, h) for h in range(1, max(root, pairs - 1 - root) + 1)]
    for tick in range(len(units) + len(stages) - 1):
        for stage in reversed(range(len(stages))):
            k = tick - stage
            if 0 <= k < len(units):
                for d in range(2):
                    stages[stage](k, d)
        if tick < len(kv_order):
            kv_step(kv_order[tick])

    if kv:
        items = [(mate, (m,), 0, 0)]
        for k in range(1, pairs):
            kv_send(k).wait_recv()
            items.append((far, (k - 1,), 0, 0))
        add_into((dout, (), 0, 0), items, token_rows, token_cols)
        for k in range(pairs):
            kv_swap(k).wait_send()
            if k:
                kv_send(k).wait_send()
    for k in range(len(units)):
        for d in range(2):
            for j in range(n):
                swap(k, d, j).wait_send()
    for k in range(len(units)):
        for d in range(2):
            for t in range(n - 1):
                ring(k, d, t).wait_send()

            @pl.when(m != root)
            def _():
                climb(k, d).wait_send()

            @pl.when((m > 0) & (m <= root))
            def _():
                share(k, d, 0).wait_send()

            @pl.when((m >= root) & (m < pairs - 1))
            def _():
                share(k, d, 1).wait_send()

            twin(k, d).wait()


def scatter(n, pairs, cid, grads, kv=None):
    nw = len(grads)
    units = []
    for i, g in enumerate(grads):
        width = g.shape[2] // 2
        pieces = 3 if width % 384 == 0 and width * g.shape[1] >= 200000 else 1
        units += [(i, j, width // pieces) for j in range(pieces)]
    args = list(grads)
    shapes = [jax.ShapeDtypeStruct(g.shape[1:], BF16) for g in grads]
    vm = pltpu.VMEM
    halves = [(g.shape[1] // 2, g.shape[2]) for g in grads]
    scratch = [vm((n,) + h, BF16) for h in halves] * 2
    scratch += [vm((n - 1,) + h, BF16) for h in halves]
    scratch += [vm(h, BF16) for h in halves] * 2
    dma = pltpu.SemaphoreType.DMA
    both = 2 * len(units)
    sems = [dma((both * n,))] * 2 + [dma((both * (n - 1),))] * 2 + [dma((both,))] * 3
    sems += [dma((2 * both,)), dma((both,)), dma((both,)), dma((both,))]
    if kv is not None:
        args.append(kv)
        shapes.append(jax.ShapeDtypeStruct(kv.shape[1:], F32))
        scratch += [vm((pairs,) + kv.shape[1:], BF16), vm((pairs - 1,) + kv.shape[1:], BF16)]
        sems += [dma((pairs,))] * 4
    outs = pl.pallas_call(
        functools.partial(scatter_kernel, n, pairs, nw, tuple(units), kv is not None),
        out_shape=shapes,
        in_specs=[pl.BlockSpec(memory_space=pltpu.VMEM)] * len(args),
        out_specs=[pl.BlockSpec(memory_space=pltpu.VMEM)] * len(args),
        scratch_shapes=scratch + sems,
        compiler_params=pltpu.CompilerParams(
            collective_id=cid, has_side_effects=True, vmem_limit_bytes=VMEM_LIMIT
        ),
        name=f"scatter{cid}",
    )(*args)
    return list(outs)


def lanes(ref):
    return jnp.concatenate([ref[j] for j in range(ref.shape[0])], axis=1)


def attend_kernel(scale, q_ref, k_ref, v_ref, valid_ref, ctx_ref, lse_ref):
    scores = contract_dims(q_ref[...], lanes(k_ref), 0, 0) * scale
    scores = jnp.where(valid_ref[...] > 0, scores, -1e30)
    peak = jnp.max(scores, axis=1, keepdims=True)
    weight = jnp.exp(scores - peak)
    norm = jnp.sum(weight, axis=1, keepdims=True)
    lse_ref[0] = peak + jnp.log(norm)
    probs = (weight * (1.0 / norm)).astype(BF16)
    ctx_ref[...] = contract_dims(lanes(v_ref), probs, 1, 1)


def attend(scale, query_t, kv, valid):
    width, toks = query_t.shape
    size = width // HEADS
    blocks = kv.shape[0]
    return pl.pallas_call(
        functools.partial(attend_kernel, scale),
        grid=(HEADS,),
        out_shape=(
            jax.ShapeDtypeStruct((width, toks), F32),
            jax.ShapeDtypeStruct((HEADS, toks, 1), F32),
        ),
        in_specs=[
            pl.BlockSpec((size, toks), lambda h: (h, 0)),
            pl.BlockSpec((blocks, size, toks), lambda h: (0, h, 0)),
            pl.BlockSpec((blocks, size, toks), lambda h: (0, HEADS + h, 0)),
            pl.BlockSpec(valid.shape, lambda h: (0, 0)),
        ],
        out_specs=(
            pl.BlockSpec((size, toks), lambda h: (h, 0)),
            pl.BlockSpec((1, toks, 1), lambda h: (h, 0, 0)),
        ),
        compiler_params=pltpu.CompilerParams(vmem_limit_bytes=VMEM_LIMIT // 2),
        name="attend",
    )(query_t, kv, kv, valid)


def attend_back_kernel(
    scale, q_ref, k_ref, v_ref, valid_ref, lse_ref, dctx_ref, ctx_ref, dq_ref, dk_ref, dv_ref
):
    query, keys, values = q_ref[...], lanes(k_ref), lanes(v_ref)
    dctx = dctx_ref[...]
    dctx_b = dctx.astype(BF16)
    delta_row = jnp.sum(dctx * ctx_ref[...], axis=0, keepdims=True)
    delta = jnp.transpose(jnp.broadcast_to(delta_row, (8, delta_row.shape[1])))[:, :1]
    scores = contract_dims(query, keys, 0, 0) * scale
    scores = jnp.where(valid_ref[...] > 0, scores, -1e30)
    prob = jnp.exp(scores - lse_ref[0])
    dvalue = jnp.dot(dctx_b, prob.astype(BF16), preferred_element_type=F32)
    dprob = contract_dims(dctx_b, values, 0, 0)
    dscore = (prob * (dprob - delta)).astype(BF16)
    dq_ref[...] = contract_dims(keys, dscore, 1, 1) * scale
    dkey = jnp.dot(query, dscore, preferred_element_type=F32) * scale
    toks = query.shape[1]
    for j in range(dk_ref.shape[0]):
        dk_ref[j] = dkey[:, j * toks : (j + 1) * toks].astype(BF16)
        dv_ref[j] = dvalue[:, j * toks : (j + 1) * toks].astype(BF16)


def attend_back(scale, query_t, kv, valid, lse, dctx_t, ctx_t):
    width, toks = query_t.shape
    size = width // HEADS
    blocks = kv.shape[0]
    head = pl.BlockSpec((size, toks), lambda h: (h, 0))
    keys = pl.BlockSpec((blocks, size, toks), lambda h: (0, h, 0))
    return pl.pallas_call(
        functools.partial(attend_back_kernel, scale),
        grid=(HEADS,),
        out_shape=(
            jax.ShapeDtypeStruct((width, toks), F32),
            jax.ShapeDtypeStruct((blocks, width, toks), BF16),
            jax.ShapeDtypeStruct((blocks, width, toks), BF16),
        ),
        in_specs=[
            head,
            keys,
            pl.BlockSpec((blocks, size, toks), lambda h: (0, HEADS + h, 0)),
            pl.BlockSpec(valid.shape, lambda h: (0, 0)),
            pl.BlockSpec((1, toks, 1), lambda h: (h, 0, 0)),
            head,
            head,
        ],
        out_specs=(head, keys, keys),
        compiler_params=pltpu.CompilerParams(vmem_limit_bytes=VMEM_LIMIT // 2),
        name="attend_back",
    )(query_t, kv, kv, valid, lse, dctx_t, ctx_t)


def local(
    n,
    n_ctx,
    tokens,
    lengths,
    cotangent,
    w_qkv,
    b_query,
    b_value,
    w_out,
    b_out,
    ln1_gain,
    ln1_bias,
    w_up,
    b_up,
    w_down,
    b_down,
    ln2_gain,
    ln2_bias,
):
    pairs = n_ctx // 2
    x = tokens[0]
    toks, width = x.shape
    scale = 1.0 / math.sqrt(width // HEADS)
    limit = lengths[0]
    vectors = (b_query, b_value, b_out, ln1_gain, ln1_bias, b_down, ln2_gain, ln2_bias, b_up)
    lens = [v.shape[0] for v in vectors]
    lane = 256
    rows = -(-sum(lens) // lane)
    rows = -(-rows // 32) * 32
    base = min(lens)
    flat = jnp.concatenate([v.astype(F32).reshape(-1, base) for v in vectors])
    flat = jnp.pad(flat, ((0, -flat.shape[0] % 8), (0, -base % 128)))
    wq_all, small_all = gather(n, pairs, 0, [w_qkv], small=flat)
    wq_full = wq_all.reshape(width, -1)
    parts, at = [], 0
    for size in lens:
        parts.append(small_all[:, at : at + size // base, :base].reshape(-1))
        at += size // base
    bq, bv, bo, g1, c1, bd, g2, c2, bu = parts

    qkv_t = contract_dims(wq_full, x, 0, 1)
    query_t = (qkv_t[:width] + bq[:, None]).astype(BF16)
    shift = jnp.concatenate([jnp.zeros((width,), F32), bv])
    kv_t = (qkv_t[width:] + shift[:, None]).astype(BF16)
    wo_all, wu_all, wd_all, kv = gather(n, pairs, 1, [w_out, w_up, w_down], kv=kv_t)
    wo_full = wo_all.reshape(width, -1)
    wu_full = wu_all.reshape(width, -1)
    wd_full = wd_all.reshape(-1, width)
    valid = (jnp.arange(n_ctx * toks, dtype=jnp.int32) < limit).astype(F32)[None, :]

    ctx_t, lse = attend(scale, query_t, kv, valid)
    context_b_t = ctx_t.astype(BF16)
    z_one = x.astype(F32) + contract_dims(context_b_t, wo_full, 0, 0) + bo
    n_one, rstd_one = normalize(z_one)
    x_one = n_one * g1 + c1
    x_one_b = x_one.astype(BF16)
    upper = jnp.dot(x_one_b, wu_full, preferred_element_type=F32) + bu
    hidden_f, gelu_back = jax.vjp(gelu_exact, upper)
    hidden = hidden_f.astype(BF16)
    z_two = x_one + jnp.dot(hidden, wd_full, preferred_element_type=F32) + bd
    n_two, rstd_two = normalize(z_two)
    out = (n_two * g2 + c2).astype(BF16)
    grad = cotangent[0].astype(F32)
    dg_two = jnp.sum(grad * n_two, axis=0)
    db_two = jnp.sum(grad, axis=0)
    dz_two = norm_back(grad * g2, n_two, rstd_two)
    dz_two_b = dz_two.astype(BF16)
    dw_down = contract_dims(hidden, dz_two_b, 0, 0)
    db_down = jnp.sum(dz_two, axis=0)
    dhid = contract_dims(dz_two_b, wd_full, 1, 1)
    dupper = gelu_back(dhid)[0]
    dupper_b = dupper.astype(BF16)
    dw_up = contract_dims(x_one_b, dupper_b, 0, 0)
    db_up = jnp.sum(dupper, axis=0)
    dx_one = dz_two + contract_dims(dupper_b, wu_full, 1, 1)
    dg_one = jnp.sum(dx_one * n_one, axis=0)
    db_one = jnp.sum(dx_one, axis=0)
    dz_one = norm_back(dx_one * g1, n_one, rstd_one)
    dz_one_b = dz_one.astype(BF16)
    dw_out = contract_dims(context_b_t, dz_one_b, 1, 0)
    db_out = jnp.sum(dz_one, axis=0)
    dctx_t = contract_dims(wo_full, dz_one_b, 1, 1)

    query_grad_t, dkeys, dvalues = attend_back(scale, query_t, kv, valid, lse, dctx_t, ctx_t)
    dkv = jnp.concatenate([dkeys, dvalues], axis=1)

    def blocks(g):
        return g.astype(BF16).reshape(n, -1, g.shape[1])

    up_sum, down_sum, out_sum, kv_grad_t = scatter(
        n, pairs, 2, [blocks(dw_up), blocks(dw_down), blocks(dw_out)], kv=dkv
    )
    dqkv_b_t = jnp.concatenate([query_grad_t.astype(BF16), kv_grad_t.astype(BF16)], axis=0)
    dw_qkv = contract_dims(x, dqkv_b_t, 0, 1)
    dx = dz_one + contract_dims(dqkv_b_t, wq_full, 0, 1)
    db_query = jnp.sum(query_grad_t, axis=1)
    db_value = jnp.sum(kv_grad_t[width:], axis=1)
    small_grads = (db_query, db_value, db_out, dg_one, db_one, db_down, dg_two, db_two, db_up)
    packed = jnp.concatenate([g.astype(BF16).reshape(n, -1) for g in small_grads], axis=1)
    packed = jnp.pad(packed, ((0, 0), (0, rows * lane - packed.shape[1]))).reshape(n, rows, lane)
    qkv_sum, small_sum = scatter(n, pairs, 3, [blocks(dw_qkv), packed])
    small_sum = small_sum.reshape(rows * lane).astype(F32)
    pieces, at = [], 0
    for size in lens:
        pieces.append(small_sum[at : at + size])
        at += size
    gq, gv, go, gg1, gc1, gd, gg2, gc2, gu = pieces
    return (
        out[None],
        dx[None],
        qkv_sum.astype(F32),
        gq,
        gv,
        out_sum.astype(F32),
        go,
        gg1,
        gc1,
        up_sum.astype(F32),
        gu,
        down_sum.astype(F32),
        gd,
        gg2,
        gc2,
    )


def solution(mesh):
    rows, blocks, flat = P("shard", None), P("shard", "ctx", None), P("shard")
    in_specs = (
        blocks, flat, blocks, rows, flat, flat, rows, flat, flat, flat, rows, flat, rows, flat, flat, flat,
    )
    out_specs = (
        blocks, blocks, rows, flat, flat, rows, flat, flat, flat, rows, flat, rows, flat, flat, flat,
    )
    body = functools.partial(local, mesh.shape["shard"], mesh.shape["ctx"])
    return jax.shard_map(body, mesh=mesh, in_specs=in_specs, out_specs=out_specs, check_vma=False)
```
